32 devices in a mesh: src: 8 (over z, y), freq: 4 (over x, core).
Axes of the slice: x: 2, y: 2, z: 4, core: 2. Of those that a mesh axis runs over, the one named last changes fastest.
Arguments:
- reflection: bfloat16 [2, 16, 2304, 2304], P(None, 'freq', 'src'), may hold values from -0.09375 to 0.09375
- focusing: bfloat16 [2, 16, 2304, 128], P(None, 'freq', 'src'), may hold values from -6 to 6
- direct_field: float32 [32, 2304, 128], P('freq', 'src'), may hold values from -6 to 6
- onset_index: int32 [2304, 128], P('src'), may hold values from 1 to 15
- end_index: int32 [2304, 128], P('src'), may hold values from 17 to 31
Outputs:
- updated: float32 [32, 2304, 128], P('freq', 'src')
The draws below stay inside these ranges and needn't reach their ends.
Inputs may be any that keep to these rules, and one draw needn't show every extreme that they name: `onset_index`: each trace's onset lies before the middle sample. `end_index`: each trace's window ends after the middle sample.
All inputs are finite; a program needn't handle non-finite values.
Results may differ from the reference program's by a relative error of at most 0.0003.
Values may be sent and summed in bfloat16 or wider, within the bound.
No kernel may reach another device: no remote copies, remote signals or barrier semaphores. Data moves between devices by JAX's collectives and lax.ppermute only.
A program may use at most 64 MiB of HBM per device.

```python
import math
import jax
import jax.numpy as jnp
from jax import lax

NR = 2304
NS = 2304
NP = 128
RESIDUES = 4
FREQS = 16
NT = 32


def with_ends(entries, key, least, top_value):
    place = [jax.random.randint(jax.random.fold_in(key, axis), (), 0, length) for axis, length in enumerate(entries.shape)]
    longest = entries.shape.index(max(entries.shape))
    next_to = place[:longest] + [(place[longest] + 1) % entries.shape[longest]] + place[longest + 1:]
    return entries.at[tuple(place)].set(least).at[tuple(next_to)].set(top_value)


def levels(own_key, extent, shards, low, high):
    def one(dim, parts):
        steps = jax.random.uniform(jax.random.fold_in(jax.random.fold_in(own_key, 6), dim), (parts,), jnp.float32, low / len(shards), high / len(shards))
        return jnp.repeat(jnp.exp(steps), extent[dim] // parts).reshape((-1,) + (1,) * (len(extent) - dim - 1))

    gain = one(*shards[0])
    for cut in shards[1:]:
        gain = gain * one(*cut)
    return gain


def gaussian(own_key, shape, width, bound, split=(), kind=jnp.bfloat16):
    drawn = width * jax.random.normal(own_key, shape, jnp.float32)
    if split:
        drawn = drawn * levels(own_key, shape, split, -0.22, 0.18)
    return jnp.clip(drawn, -bound, bound).astype(kind)


def setup_inputs(seed: int = 0) -> dict:
    keys = jax.random.split(jax.random.key(seed), 6)
    return {
        "reflection": gaussian(keys[0], (2, FREQS, NR, NS), (2 * NS) ** -0.5, 0.09375, ((1, 4), (2, 8))),
        "focusing": gaussian(keys[1], (2, FREQS, NS, NP), 1.0, 6.0, ((1, 4), (2, 8))),
        "direct_field": gaussian(keys[2], (NT, NR, NP), 1.0, 6.0, ((0, 4), (1, 8)), jnp.float32),
        "onset_index": with_ends(jax.random.randint(keys[3], (NR, NP), 1, NT // 2), jax.random.fold_in(keys[3], 1), 1, (NT // 2) - 1).astype(jnp.int32),
        "end_index": with_ends(jax.random.randint(keys[4], (NR, NP), NT // 2 + 1, NT), jax.random.fold_in(keys[4], 1), NT // 2 + 1, NT - 1).astype(jnp.int32),
    }


def reverse_bits(values, bit_count):
    result = jnp.zeros_like(values)
    for bit_index in range(bit_count):
        result = result + values // 2 ** bit_index % 2 * 2 ** (bit_count - 1 - bit_index)
    return result

def reference(reflection, focusing, direct_field, onset_index, end_index):
    freq_total = reflection.shape[1]
    sample_total = 2 * freq_total
    bit_count = RESIDUES.bit_length() - 1
    per_device = freq_total // RESIDUES

    def one_frequency(freq_row):
        matrix = lax.dynamic_index_in_dim(reflection, freq_row, 1, keepdims=False)
        vector = lax.dynamic_index_in_dim(focusing, freq_row, 1, keepdims=False)
        real_part = jnp.dot(matrix[0], vector[0], preferred_element_type=jnp.float32) - jnp.dot(matrix[1], vector[1], preferred_element_type=jnp.float32)
        imag_part = jnp.dot(matrix[0], vector[1], preferred_element_type=jnp.float32) + jnp.dot(matrix[1], vector[0], preferred_element_type=jnp.float32)
        return jnp.stack((real_part, imag_part))
    freq_rows = jnp.arange(freq_total, dtype=jnp.int32)
    spectrum = lax.map(one_frequency, freq_rows)
    frequency = freq_rows % per_device * RESIDUES + reverse_bits(freq_rows // per_device, bit_count)
    samples = jnp.arange(sample_total, dtype=jnp.int32)
    phase_index = samples[:, None] * frequency[None, :] % sample_total
    twiddle_angle = phase_index.astype(jnp.float32) * (2.0 * math.pi / sample_total)
    norm_factor = 1.0 / math.sqrt(freq_total)
    trace = (jnp.einsum('sq,qrn->srn', jnp.cos(twiddle_angle), spectrum[:, 0], precision=lax.Precision.HIGHEST) - jnp.einsum('sq,qrn->srn', jnp.sin(twiddle_angle), spectrum[:, 1], precision=lax.Precision.HIGHEST)) * norm_factor
    window = (samples[:, None, None] >= onset_index[None]) & (samples[:, None, None] < end_index[None])
    muted = jnp.where(window, trace, jnp.float32(0.0))
    reversed_trace = jnp.roll(jnp.flip(muted, 0), 1, 0)
    return direct_field - reversed_trace
```

```python
import math

import jax
import jax.numpy as jnp
from jax import lax
from jax.experimental import pallas as pl
from jax.experimental.pallas import tpu as pltpu
from jax.sharding import PartitionSpec as P


def reverse_bits(values, bit_count):
    result = jnp.zeros_like(values)
    for bit_index in range(bit_count):
        result = result + values // 2**bit_index % 2 * 2 ** (bit_count - 1 - bit_index)
    return result


def ring_order(count):
    return list(range(0, count, 2)) + [i for i in range(count - 1, 0, -1) if i % 2]


def row_product(row, sources, reflection, focusing, blocks):
    receivers, source_total = reflection.shape[2], reflection.shape[3]
    block_rows, points = focusing.shape[2], focusing.shape[3]
    count = len(blocks)

    def body(sources_ref, refl_ref, foc_ref, *rest):
        block_refs = rest[:count]
        out_ref, refl_buf, foc_buf, refl_sem, foc_sem = rest[count:]
        refl_copies = [
            pltpu.make_async_copy(refl_ref.at[part, row], refl_buf.at[part], refl_sem.at[part])
            for part in range(2)
        ]
        foc_copies = []

        def place(src, index, part, sem):
            start = pl.multiple_of(sources_ref[index] * block_rows, block_rows)
            return pltpu.make_async_copy(
                src,
                foc_buf.at[pl.ds(start, block_rows), pl.ds(part * points, points)],
                foc_sem.at[sem],
            )

        for part in range(2):
            foc_copies.append(place(foc_ref.at[part, row], 0, part, len(foc_copies)))
        for ref, (_, index, part) in zip(block_refs, blocks):
            if part is None:
                for one in range(2):
                    foc_copies.append(place(ref.at[one], index, one, len(foc_copies)))
            else:
                foc_copies.append(place(ref, index, part, len(foc_copies)))
        for copy in refl_copies + foc_copies:
            copy.start()
        for copy in foc_copies:
            copy.wait()
        refl_copies[0].wait()
        first = jnp.dot(refl_buf[0], foc_buf[...], preferred_element_type=jnp.float32)
        refl_copies[1].wait()
        second = jnp.dot(refl_buf[1], foc_buf[...], preferred_element_type=jnp.float32)
        out_ref[0] = first[:, :points] - second[:, points:]
        out_ref[1] = first[:, points:] + second[:, :points]

    any_spec = pl.BlockSpec(memory_space=pl.ANY)
    return pl.pallas_call(
        body,
        out_shape=jax.ShapeDtypeStruct((2, receivers, points), jnp.float32),
        grid_spec=pltpu.PrefetchScalarGridSpec(
            num_scalar_prefetch=1,
            grid=(1,),
            in_specs=[any_spec] * (2 + count),
            out_specs=pl.BlockSpec((2, receivers, points), lambda i, s: (0, 0, 0)),
            scratch_shapes=[
                pltpu.VMEM((2, receivers, source_total), reflection.dtype),
                pltpu.VMEM((source_total, 2 * points), focusing.dtype),
                pltpu.SemaphoreType.DMA((2,)),
                pltpu.SemaphoreType.DMA((2 * count + 2,)),
            ],
        ),
        name="row_product",
    )(sources, reflection, focusing, *[array for array, _, _ in blocks])


def subtract_muted(base, spectra, weights, onset, end, source_sample):
    samples, receivers, points = base.shape
    count = len(spectra)
    tile = 16
    block = receivers // 2 if receivers % (2 * tile) == 0 else receivers

    def body(weight_ref, sample_ref, onset_ref, end_ref, base_ref, *rest):
        spectrum_refs, out_ref = rest[:count], rest[count]

        def one_tile(index, carry):
            rows = pl.ds(pl.multiple_of(index * tile, tile), tile)
            totals = [None] * samples
            for place, ref in enumerate(spectrum_refs):
                for part in range(2):
                    value = ref[part, rows, :]
                    for sample in range(samples):
                        term = value * weight_ref[(place * 2 + part) * samples + sample]
                        totals[sample] = term if totals[sample] is None else totals[sample] + term
            first, last = onset_ref[rows, :], end_ref[rows, :]
            for sample in range(samples):
                at = sample_ref[sample]
                keep = (at >= first) & (at < last)
                out_ref[sample, rows, :] = base_ref[sample, rows, :] - jnp.where(
                    keep, totals[sample], jnp.float32(0.0)
                )
            return carry

        lax.fori_loop(0, block // tile, one_tile, 0)

    smem = pl.BlockSpec(memory_space=pltpu.SMEM)
    window_spec = pl.BlockSpec((block, points), lambda i: (i, 0))
    base_spec = pl.BlockSpec((samples, block, points), lambda i: (0, i, 0))
    spectrum_spec = pl.BlockSpec((2, block, points), lambda i: (0, i, 0))
    return pl.pallas_call(
        body,
        out_shape=jax.ShapeDtypeStruct(base.shape, jnp.float32),
        grid=(receivers // block,),
        in_specs=[smem, smem, window_spec, window_spec, base_spec] + [spectrum_spec] * count,
        out_specs=base_spec,
        name="subtract_muted",
    )(weights.reshape(-1), source_sample, onset, end, base, *spectra)


def per_device(reflection, focusing, direct_field, onset_index, end_index):
    freqs_dev = reflection.shape[1]
    block_samples = direct_field.shape[0]
    group_size = lax.axis_size("freq")
    src_size = lax.axis_size("src")
    bit_count = group_size.bit_length() - 1
    device_index = lax.axis_index("freq")
    freq_total = freqs_dev * group_size
    sample_total = 2 * freq_total
    norm_factor = 1.0 / math.sqrt(freq_total)

    order = ring_order(src_size)
    to_right = [(order[i], order[(i + 1) % src_size]) for i in range(src_size)]
    to_left = [(b, a) for a, b in to_right]
    full_steps = (src_size - 1) // 2
    src_index = lax.axis_index("src")
    half_up = (src_size + 1) // 2
    ring_place = jnp.where(src_index % 2 == 0, src_index // 2, src_size - 1 - src_index // 2)
    offsets = [0]
    for step in range(1, full_steps + 1):
        offsets += [-step, step]
    if src_size % 2 == 0:
        offsets.append(src_size // 2)
    places = (ring_place + jnp.array(offsets, jnp.int32) + src_size) % src_size
    sources = jnp.where(
        places < half_up, 2 * places, 2 * (src_size - 1 - places) + 1
    ).astype(jnp.int32)

    cores = 2 if group_size % 2 == 0 else 1
    chips = group_size // cores
    to_chip = [(i, (i + cores) % group_size) for i in range(group_size)]
    to_core = [(i, i ^ 1) for i in range(group_size)]

    spectra = []
    for row in range(freqs_dev):
        own = focusing[:, row]
        rightward = leftward = own
        blocks = []
        for step in range(1, full_steps + 1):
            rightward = lax.ppermute(rightward, "src", to_right)
            leftward = lax.ppermute(leftward, "src", to_left)
            blocks.append((rightward, 2 * step - 1, None))
            blocks.append((leftward, 2 * step, None))
        if src_size % 2 == 0:
            blocks.append((lax.ppermute(rightward[0], "src", to_right), len(offsets) - 1, 0))
            blocks.append((lax.ppermute(leftward[1], "src", to_left), len(offsets) - 1, 1))
        spectrum = row_product(row, sources, reflection, focusing, blocks)
        held = []
        moving = spectrum
        for hop in range(chips):
            if hop:
                moving = lax.ppermute(moving, "freq", to_chip)
            place = (device_index - cores * hop) % group_size
            held.append((moving, place))
            if cores == 2:
                held.append((lax.ppermute(moving, "freq", to_core), place ^ 1))
        spectra.append(held)

    sample_rows = device_index * block_samples + jnp.arange(block_samples, dtype=jnp.int32)
    source_sample = (sample_total - sample_rows) % sample_total

    def weights(row, places):
        frequency = row * group_size + reverse_bits(jnp.stack(places), bit_count)
        phase = (source_sample[None, :] * frequency[:, None]) % sample_total
        angle = phase.astype(jnp.float32) * (2.0 * math.pi / sample_total)
        return jnp.stack((jnp.cos(angle), -jnp.sin(angle)), 1) * norm_factor

    updated = direct_field
    for row in range(freqs_dev):
        held = spectra[row]
        updated = subtract_muted(
            updated,
            [array for array, _ in held],
            weights(row, [place for _, place in held]),
            onset_index,
            end_index,
            source_sample,
        )
    return updated


def solution(mesh):
    placed = (
        P(None, "freq", "src", None),
        P(None, "freq", "src", None),
        P("freq", "src", None),
        P("src", None),
        P("src", None),
    )
    return jax.shard_map(
        per_device, mesh=mesh, in_specs=placed, out_specs=P("freq", "src", None), check_vma=False
    )
```
